32 devices in a mesh: groups: 2 (over x), req: 8 (over z, core), row: 2 (over y).
Axes of the slice: x: 2, y: 2, z: 4, core: 2. Of those that a mesh axis runs over, the one named last changes fastest.
Arguments:
- latents: bfloat16 [16, 2, 4, 2560], P('groups', None, 'row', 'req'), parts along dimension 0, may hold values from -8 to 8
- dispatch_plan: int32 [16], P('groups'), parts along dimension 0, may hold values from 0 to 7, each once
- span_counts: int32 [8], P('groups'), parts along dimension 0, may hold values from 1 to 4, 8 in all
- in_weight: bfloat16 [432, 384], replicated, may hold values from -0.3125 to 0.3125
- in_bias: float32 [384], replicated, may hold values from -3 to 3
- norm_gain: float32 [384], replicated, may hold values from 0.5 to 1.5
- norm_bias: float32 [384], replicated, may hold values from -3 to 3
- mid_weight: bfloat16 [27, 384, 384], replicated, may hold values from -0.0625 to 0.0625
- mid_bias: float32 [384], replicated, may hold values from -3 to 3
Outputs:
- decoded: bfloat16 [16, 2, 4, 61440], P(('groups', 'req'), None, 'row'), parts along dimension 0
The draws below stay inside these ranges and needn't reach their ends.
There are 2 independent parts, one for each index of `groups`. The reference program is written for one: setup_inputs(seed, part) draws one part's arguments, and reference() takes and returns one part's arrays. A program takes and returns all parts, laid end to end along the dimension named above; an argument that names none is the same for every part. Nothing has to cross between parts.
Inputs may be any that keep to these rules, and one draw needn't show every extreme that they name: `span_counts`: the counts sum to 8.
All inputs are finite; a program needn't handle non-finite values.
Results may differ from the reference program's by a relative error of at most 0.0029.
Values may be sent and summed in bfloat16 or wider, within the bound.
A program may use at most 64 MiB of HBM per device.

```python
import math
import jax
import jax.numpy as jnp
import numpy as np
from jax import lax

C = 384
C_LAT = 16
G = 32
CF = 2
W = 160
H = 4
REQS = 4
MOST = 4
N_REQ = 8


def draw_latents(key, part):
    full_shape = (N_REQ, CF, H, W * C_LAT)
    row_place = jnp.arange(H, dtype=jnp.float32) / max(H - 1, 1)
    row_scale = 0.6 * jnp.exp(row_place * math.log(3.0))
    values = jax.random.normal(key, full_shape, jnp.float32) * row_scale[None, None, :, None]
    return jnp.clip(values, -8.0, 8.0).astype(jnp.bfloat16)


def split_up(amount, total, most, skew):
    portions = [(1 << 20) // math.isqrt(rank ** skew) + 1 for rank in range(2, amount + 1)]
    surplus, holding = total - most - (amount - 1), [1] * (amount - 1)
    while surplus > 0:
        candidates = [i for i in range(amount - 1) if holding[i] < most]
        whole, remaining = sum([portions[i] for i in candidates]), surplus
        for i in candidates:
            more = min(most - holding[i], max(1, remaining * portions[i] // whole), surplus)
            holding[i] = holding[i] + more
            surplus = surplus - more
    return np.array([most] + holding)


def uneven(key, count, total, bound, skew):
    if count == 2:
        one = jax.random.randint(key, (), max(1, total - bound), min(bound, total - 1) + 1)
        return jnp.stack([one, total - one])
    lengths = jnp.asarray(split_up(count, total, bound, skew), jnp.int32)
    twos = (count - 1) // 2
    source_of, receiver = lengths[1:1 + 2 * twos:2], lengths[2:2 + 2 * twos:2]
    room = jnp.minimum(source_of - 1, bound - receiver)
    shifted = jax.random.randint(jax.random.fold_in(key, 1), (twos,), 0, 1 << 20) % (room + 1)
    lengths = lengths.at[1:1 + 2 * twos:2].set(source_of - shifted).at[2:2 + 2 * twos:2].set(receiver + shifted)
    return lengths[jax.random.permutation(jax.random.fold_in(key, 2), count)]


def normal_values(rng, shape, scale, limit, kind=jnp.bfloat16):
    values = jax.random.normal(rng, shape, jnp.float32) * scale
    return jnp.minimum(jnp.maximum(values, -limit), limit).astype(kind)


def setup_inputs(seed: int = 0, part: int = 0) -> dict:
    splits = jax.random.split(jax.random.key(seed), 10)
    own_keys = jax.random.split(jax.random.fold_in(splits[9], part), 10)
    return {
        "latents": draw_latents(jax.random.fold_in(jax.random.fold_in(splits[9], part), 71), part),
        "dispatch_plan": jax.random.permutation(own_keys[1], N_REQ).astype(jnp.int32),
        "span_counts": uneven(own_keys[2], REQS, N_REQ, MOST, 2).astype(jnp.int32),
        "in_weight": normal_values(splits[3], (27 * C_LAT, C), (27 * C_LAT) ** -0.5, 0.3125),
        "in_bias": normal_values(splits[4], (C,), 0.5, 3.0, jnp.float32),
        "norm_gain": jnp.clip(jax.random.uniform(splits[5], (C,), jnp.float32, 0.5, 1.5), 0.5, 1.5),
        "norm_bias": normal_values(splits[6], (C,), 0.5, 3.0, jnp.float32),
        "mid_weight": normal_values(splits[7], (27, C, C), (27 * C) ** -0.5, 0.0625),
        "mid_bias": normal_values(splits[8], (C,), 0.5, 3.0, jnp.float32),
    }


def conv_input(frames, in_weight):
    frame_total, row_total, col_total, chans = frames.shape
    padded = jnp.pad(frames, ((0, 0), (0, 0), (1, 1), (0, 0)))
    out_frames = frame_total - 2
    out_rows = row_total - 2
    tap_list = []
    for time_off in range(3):
        for row_off in range(3):
            for col_off in range(3):
                tap_list.append(padded[time_off:time_off + out_frames, row_off:row_off + out_rows, col_off:col_off + col_total, :])
    stacked = jnp.concatenate(tap_list, axis=-1).reshape(-1, 27 * chans)
    result = jnp.dot(stacked, in_weight, preferred_element_type=jnp.float32)
    return result.reshape(out_frames, out_rows, col_total, in_weight.shape[1])

def conv_hidden(frames, mid_weight):
    frame_total, row_total, col_total, chans = frames.shape
    padded = jnp.pad(frames, ((0, 0), (0, 0), (1, 1), (0, 0)))
    out_frames = frame_total - 2
    out_rows = row_total - 2
    running = jnp.zeros((out_frames * out_rows * col_total, mid_weight.shape[2]), jnp.float32)
    for time_off in range(3):
        for row_off in range(3):
            for col_off in range(3):
                tap_rows = padded[time_off:time_off + out_frames, row_off:row_off + out_rows, col_off:col_off + col_total, :].reshape(-1, chans)
                running = running + jnp.dot(tap_rows, mid_weight[(time_off * 3 + row_off) * 3 + col_off], preferred_element_type=jnp.float32)
    return running.reshape(out_frames, out_rows, col_total, mid_weight.shape[2])

def group_stats(hidden, groups):
    frame_total = hidden.shape[0]
    grouped = hidden.reshape(frame_total, -1, groups, hidden.shape[3] // groups)
    return (lax.optimization_barrier(jnp.sum(grouped, axis=(1, 3))), lax.optimization_barrier(jnp.sum(grouped * grouped, axis=(1, 3))))

def normalize(hidden, group_sums, squares, cell_count, norm_gain, norm_bias, groups):
    per_group = hidden.shape[3] // groups
    mean_val = group_sums / cell_count
    var_val = squares / cell_count - mean_val * mean_val
    inverse = lax.rsqrt(var_val + 1e-06)
    mean_chan = jnp.repeat(mean_val, per_group, axis=-1)[:, None, None, :]
    inv_chan = jnp.repeat(inverse, per_group, axis=-1)[:, None, None, :]
    normed = (hidden - mean_chan) * inv_chan * norm_gain + norm_bias
    return jax.nn.silu(normed).astype(jnp.bfloat16)

def reference(latents, dispatch_plan, span_counts, in_weight, in_bias, norm_gain, norm_bias, mid_weight, mid_bias):
    spans = jnp.take(latents, dispatch_plan, axis=0)
    starts = jnp.cumsum(span_counts) - span_counts
    first_flag = jnp.any(jnp.arange(N_REQ, dtype=jnp.int32)[:, None] == starts[None, :], axis=1)
    keep_prev = jnp.where(first_flag, 0.0, 1.0).astype(jnp.bfloat16)
    previous = jnp.concatenate([jnp.zeros_like(spans[:1]), spans[:-1]], axis=0) * keep_prev[:, None, None, None]
    extended = jnp.concatenate([previous, spans], axis=1)
    extended = jnp.pad(extended, ((0, 0), (0, 0), (1, 1), (0, 0)))
    extended = extended.reshape(N_REQ, 2 * CF, H + 2, W, C_LAT)
    hidden = lax.map(lambda block: conv_input(block, in_weight), extended) + in_bias
    flat_hidden = hidden.reshape(N_REQ * CF, H, W, C)
    group_sums, squares = group_stats(flat_hidden, G)
    active = normalize(flat_hidden, group_sums, squares, H * W * (C // G), norm_gain, norm_bias, G)
    active = active.reshape(N_REQ, CF, H, W * C)
    prev_active = jnp.concatenate([jnp.zeros_like(active[:1]), active[:-1]], axis=0) * keep_prev[:, None, None, None]
    cached = jnp.concatenate([prev_active, active], axis=1)
    cached = jnp.pad(cached, ((0, 0), (0, 0), (1, 1), (0, 0)))
    cached = cached.reshape(N_REQ, 2 * CF, H + 2, W, C)
    mixed = lax.map(lambda block: conv_hidden(block, mid_weight), cached) + mid_bias + hidden
    return mixed.astype(jnp.bfloat16).reshape(N_REQ, CF, H, W * C)
```

```python
import functools

import jax
import jax.numpy as jnp
from jax import lax
from jax.experimental import pallas as pl
from jax.experimental.pallas import tpu as pltpu
from jax.sharding import PartitionSpec as P

C_LAT = 16
G = 32
CF = 2
W = 160
LANES = 128
DEPTH = 3
MESH = pl.DeviceIdType.MESH


def exchange_kernel(req_n, row_n, plan_ref, lat_ref, out_ref, sel, send_sems, recv_sems):
    me_req = lax.axis_index("req")
    me_row = lax.axis_index("row")
    total = req_n * row_n
    flat = me_row * req_n + me_req
    barrier = pltpu.get_barrier_semaphore()

    def place(k):
        target = lax.rem(flat + k, total)
        return {"row": target // req_n, "req": lax.rem(target, req_n)}

    for k in range(1, total):
        pl.semaphore_signal(barrier, inc=1, device_id=place(k), device_id_type=MESH)
    for d in range(DEPTH - 1):
        sel[d] = jnp.zeros_like(sel[d])
    for d in range(req_n):
        sel[d + DEPTH - 1] = lat_ref[plan_ref[d]]
    pl.semaphore_wait(barrier, total - 1)
    copies = []
    for k in range(1, total):
        where = place(k)
        copy = pltpu.make_async_remote_copy(
            src_ref=sel.at[pl.ds(where["req"], DEPTH)],
            dst_ref=out_ref.at[me_row, me_req],
            send_sem=send_sems.at[k],
            recv_sem=recv_sems.at[k],
            device_id=where,
            device_id_type=MESH,
        )
        copy.start()
        copies.append(copy)
    out_ref[me_row, me_req] = sel[pl.ds(me_req, DEPTH)]
    for copy in copies:
        copy.wait()


def exchange(latents, plan):
    req_n = lax.axis_size("req")
    row_n = lax.axis_size("row")
    slots, frames, rows, lanes = latents.shape
    return pl.pallas_call(
        functools.partial(exchange_kernel, req_n, row_n),
        out_shape=jax.ShapeDtypeStruct((row_n, req_n, DEPTH, frames, rows, lanes), latents.dtype),
        in_specs=[
            pl.BlockSpec(memory_space=pltpu.SMEM),
            pl.BlockSpec(memory_space=pltpu.VMEM),
        ],
        out_specs=pl.BlockSpec(memory_space=pltpu.VMEM),
        scratch_shapes=[
            pltpu.VMEM((req_n + DEPTH - 1, frames, rows, lanes), latents.dtype),
            pltpu.SemaphoreType.DMA((req_n * row_n,)),
            pltpu.SemaphoreType.DMA((req_n * row_n,)),
        ],
        compiler_params=pltpu.CompilerParams(collective_id=0, has_side_effects=True),
        name="span_exchange",
    )(plan, latents)


def decode_kernel(
    rows_here,
    counts_ref,
    x_ref,
    in_w_ref,
    in_b_ref,
    gain_ref,
    nbias_ref,
    mid_b_ref,
    mid_w_hbm,
    out_ref,
    mid_w,
    in_w,
    pair_rows,
    pair_time,
    hid,
    act,
    sems,
):
    frames_in, height, blocks, _ = x_ref.shape
    chans = in_w_ref.shape[1]
    outs = frames_in - 2
    width = blocks * (LANES // C_LAT)
    me = lax.axis_index("req")
    row0 = lax.axis_index("row") * rows_here

    copies = []
    for tap in range(9):
        copy = pltpu.make_async_copy(
            mid_w_hbm.at[pl.ds(3 * tap, 3)], mid_w.at[pl.ds(3 * tap, 3)], sems.at[tap]
        )
        copy.start()
        copies.append(copy)

    def keep_of(d):
        start = jnp.int32(0)
        first = d <= 0
        for r in range(counts_ref.shape[0]):
            first = jnp.logical_or(first, start == d)
            start = start + counts_ref[r]
        return jnp.where(first, 0.0, 1.0).astype(jnp.float32)

    keep_own = keep_of(me)
    keep_prev = keep_of(me - 1)

    half = LANES // 2
    three = 3 * C_LAT
    in_w[...] = jnp.zeros_like(in_w)
    for t in range(3):
        for i in range(3):
            if i < 2:
                base = t * LANES + i * half
            else:
                base = 3 * LANES + t * half
            in_w[base : base + three, :] = in_w_ref[(3 * t + i) * three : (3 * t + i + 1) * three, :]

    zero_slab = jnp.zeros((width, LANES), jnp.bfloat16)
    for f in range(frames_in):
        pair_rows[f, 0] = zero_slab
    for f in range(frames_in + 1):
        pair_time[f, height] = zero_slab
    for y in range(height):
        pair_time[frames_in, y] = zero_slab

    place = lax.broadcasted_iota(jnp.int32, (width, LANES), 0) % 8
    lane = lax.broadcasted_iota(jnp.int32, (width, LANES), 1)
    low = jnp.logical_and(place == 0, lane < C_LAT)
    high = jnp.logical_and(place == 7, jnp.logical_and(lane >= 2 * C_LAT, lane < three))
    bits = [lax.rem(place // (1 << n), 2) == 1 for n in range(3)]
    edge = jnp.zeros((8, LANES), jnp.float32)

    @pl.loop(0, frames_in)
    def _(f):
        keep = jnp.where(f < CF, keep_prev, jnp.where(f < 2 * CF, keep_own, 1.0))

        @pl.loop(0, height)
        def _(y):
            cells = x_ref[f, y].astype(jnp.float32) * keep
            spread = jnp.broadcast_to(cells[:, None, :], (blocks, 8, LANES)).reshape(width, LANES)
            turned = jnp.where(bits[0], spread, pltpu.roll(spread, C_LAT, 1))
            turned = jnp.where(bits[1], pltpu.roll(turned, LANES - 2 * C_LAT, 1), turned)
            turned = jnp.where(bits[2], pltpu.roll(turned, LANES - 4 * C_LAT, 1), turned)
            before = jnp.concatenate([edge, turned[:-8]], axis=0)
            after = jnp.concatenate([turned[8:], edge], axis=0)
            window = jnp.where(low, before, jnp.where(high, after, turned))
            other = pltpu.roll(window, half, 1).astype(jnp.bfloat16)
            window = window.astype(jnp.bfloat16)
            pair_rows[f, y + 1, :, :half] = window[:, :half]
            pair_rows[f, y, :, half:] = other[:, half:]
            pair_time[f + 1, y, :, :half] = window[:, :half]
            pair_time[f, y, :, half:] = other[:, half:]

    sums = []
    cells = height * width
    for f in range(outs):
        taps = [
            pair_rows[f, :height],
            pair_rows[f + 1, :height],
            pair_rows[f + 2, :height],
            pair_time[f + 1, 1:],
            pair_time[f + 3, 1:],
        ]
        stacked = jnp.concatenate([tap.reshape(cells, LANES) for tap in taps], axis=1)
        hidden = jnp.dot(stacked, in_w[...], preferred_element_type=jnp.float32) + in_b_ref[...]
        hid[f] = hidden.reshape(height, width, chans)
        sums.append(jnp.sum(hidden, axis=0, keepdims=True))
        sums.append(jnp.sum(hidden * hidden, axis=0, keepdims=True))
    per_group = chans // G
    down = lax.broadcasted_iota(jnp.int32, (chans, chans), 0) // per_group
    over = lax.broadcasted_iota(jnp.int32, (chans, chans), 1) // per_group
    same = jnp.where(down == over, 1.0, 0.0).astype(jnp.float32)
    grouped = jnp.dot(
        jnp.concatenate(sums, axis=0),
        same,
        precision=lax.Precision.HIGHEST,
        preferred_element_type=jnp.float32,
    ) / (cells * per_group)

    span_rows = rows_here + 2
    for f in range(outs):
        mean = grouped[2 * f : 2 * f + 1]
        var = grouped[2 * f + 1 : 2 * f + 2] - mean * mean
        scale = lax.rsqrt(var + 1e-06) * gain_ref[...]

        @pl.loop(0, span_rows)
        def _(y, f=f, mean=mean, scale=scale):
            row = row0 + y - 1
            inside = jnp.logical_and(row >= 0, row < height)
            value = hid[f, jnp.clip(row, 0, height - 1)]
            value = (value - mean) * scale + nbias_ref[...]
            keep = jnp.where(inside, keep_own if f < CF else 1.0, 0.0)
            value = 0.5 * value * (1.0 + jnp.tanh(0.5 * value)) * keep
            nil = jnp.zeros((1, chans), jnp.float32)
            left = jnp.concatenate([nil, value[:-1]], axis=0)
            right = jnp.concatenate([value[1:], nil], axis=0)
            act[f, y, :, :chans] = left.astype(jnp.bfloat16)
            act[f, y, :, chans : 2 * chans] = value.astype(jnp.bfloat16)
            act[f, y, :, 2 * chans :] = right.astype(jnp.bfloat16)

    many = CF * rows_here * width
    total = hid[pl.ds(outs - CF, CF), pl.ds(row0, rows_here)].reshape(many, chans) + mid_b_ref[...]
    for t in range(3):
        for i in range(3):
            tap = 3 * t + i
            copies[tap].wait()
            cells_in = act[t : t + CF, i : i + rows_here].reshape(many, 3 * chans)
            weight = mid_w[3 * tap : 3 * tap + 3].reshape(3 * chans, chans)
            total = total + jnp.dot(cells_in, weight, preferred_element_type=jnp.float32)
    out_ref[...] = total.astype(jnp.bfloat16).reshape(CF, rows_here, width, chans)


def decode(counts, frames, rows_here, in_weight, in_bias, norm_gain, norm_bias, mid_weight, mid_bias):
    frames_in, height, blocks, _ = frames.shape
    chans = in_weight.shape[1]
    outs = frames_in - 2
    vmem = pl.BlockSpec(memory_space=pltpu.VMEM)
    return pl.pallas_call(
        functools.partial(decode_kernel, rows_here),
        out_shape=jax.ShapeDtypeStruct((CF, rows_here, W, chans), jnp.bfloat16),
        in_specs=[pl.BlockSpec(memory_space=pltpu.SMEM)] + [vmem] * 6 + [pl.BlockSpec(memory_space=pl.ANY)],
        out_specs=vmem,
        scratch_shapes=[
            pltpu.VMEM(mid_weight.shape, jnp.bfloat16),
            pltpu.VMEM((5 * LANES, chans), jnp.bfloat16),
            pltpu.VMEM((frames_in, height + 1, W, LANES), jnp.bfloat16),
            pltpu.VMEM((frames_in + 1, height + 1, W, LANES), jnp.bfloat16),
            pltpu.VMEM((outs, height, W, chans), jnp.float32),
            pltpu.VMEM((outs, rows_here + 2, W, 3 * chans), jnp.bfloat16),
            pltpu.SemaphoreType.DMA((9,)),
        ],
        compiler_params=pltpu.CompilerParams(vmem_limit_bytes=58 * 1024 * 1024),
        name="span_decode",
    )(
        counts,
        frames,
        in_weight,
        in_bias[None],
        norm_gain[None],
        norm_bias[None],
        mid_bias[None],
        mid_weight,
    )


def local(
    latents,
    dispatch_plan,
    span_counts,
    in_weight,
    in_bias,
    norm_gain,
    norm_bias,
    mid_weight,
    mid_bias,
):
    rows_here = latents.shape[2]
    chans = mid_weight.shape[2]
    arrived = exchange(latents, dispatch_plan)
    row_n, req_n = arrived.shape[:2]
    frames = arrived.transpose(2, 3, 0, 4, 1, 5).reshape(
        DEPTH * CF, row_n * rows_here, W * C_LAT // LANES, LANES
    )
    mixed = decode(
        span_counts, frames, rows_here, in_weight, in_bias, norm_gain, norm_bias, mid_weight, mid_bias
    )
    return mixed.reshape(1, CF, rows_here, W * chans)


def solution(mesh):
    placed = (
        P("groups", None, "row", "req"),
        P("groups"),
        P("groups"),
        P(),
        P(),
        P(),
        P(),
        P(),
        P(),
    )
    return jax.shard_map(
        local,
        mesh=mesh,
        in_specs=placed,
        out_specs=P(("groups", "req"), None, "row", None),
        check_vma=False,
    )
```

```python
import functools

import jax
import jax.numpy as jnp
from jax import lax
from jax.experimental import pallas as pl
from jax.experimental.pallas import tpu as pltpu
from jax.sharding import PartitionSpec as P

C_LAT = 16
G = 32
CF = 2
W = 160
LANES = 128
DEPTH = 3
MESH = pl.DeviceIdType.MESH


def exchange_kernel(req_n, row_n, plan_ref, lat_ref, out_ref, sel, send_sems, recv_sems):
    me_req = lax.axis_index("req")
    me_row = lax.axis_index("row")
    total = req_n * row_n
    flat = me_row * req_n + me_req
    barrier = pltpu.get_barrier_semaphore()

    def place(k):
        target = lax.rem(flat + k, total)
        return {"row": target // req_n, "req": lax.rem(target, req_n)}

    for k in range(1, total):
        pl.semaphore_signal(barrier, inc=1, device_id=place(k), device_id_type=MESH)
    for d in range(DEPTH - 1):
        sel[d] = jnp.zeros_like(sel[d])
    for d in range(req_n):
        sel[d + DEPTH - 1] = lat_ref[plan_ref[d]]
    pl.semaphore_wait(barrier, total - 1)
    copies = []
    for k in range(1, total):
        where = place(k)
        copy = pltpu.make_async_remote_copy(
            src_ref=sel.at[pl.ds(where["req"], DEPTH)],
            dst_ref=out_ref.at[me_row, me_req],
            send_sem=send_sems.at[k],
            recv_sem=recv_sems.at[k],
            device_id=where,
            device_id_type=MESH,
        )
        copy.start()
        copies.append(copy)
    out_ref[me_row, me_req] = sel[pl.ds(me_req, DEPTH)]
    for copy in copies:
        copy.wait()


def exchange(latents, plan):
    req_n = lax.axis_size("req")
    row_n = lax.axis_size("row")
    slots, frames, rows, lanes = latents.shape
    return pl.pallas_call(
        functools.partial(exchange_kernel, req_n, row_n),
        out_shape=jax.ShapeDtypeStruct((row_n, req_n, DEPTH, frames, rows, lanes), latents.dtype),
        in_specs=[
            pl.BlockSpec(memory_space=pltpu.SMEM),
            pl.BlockSpec(memory_space=pltpu.VMEM),
        ],
        out_specs=pl.BlockSpec(memory_space=pltpu.VMEM),
        scratch_shapes=[
            pltpu.VMEM((req_n + DEPTH - 1, frames, rows, lanes), latents.dtype),
            pltpu.SemaphoreType.DMA((req_n * row_n,)),
            pltpu.SemaphoreType.DMA((req_n * row_n,)),
        ],
        compiler_params=pltpu.CompilerParams(collective_id=0, has_side_effects=True),
        name="span_exchange",
    )(plan, latents)


def decode_kernel(
    rows_here,
    counts_ref,
    x_ref,
    in_w_ref,
    in_b_ref,
    gain_ref,
    nbias_ref,
    mid_b_ref,
    mid_w_hbm,
    out_ref,
    mid_w,
    in_w,
    pair_rows,
    pair_time,
    hid,
    act,
    sems,
):
    row_n, req_n = x_ref.shape[:2]
    frames_in = DEPTH * CF
    height = row_n * rows_here
    width = req_n * x_ref.shape[5] // C_LAT
    blocks = width * C_LAT // LANES
    chans = in_w_ref.shape[1]
    outs = frames_in - 2
    in_b = in_b_ref[...].reshape(1, chans)
    gain = gain_ref[...].reshape(1, chans)
    nbias = nbias_ref[...].reshape(1, chans)
    mid_b = mid_b_ref[...].reshape(1, chans)
    me = lax.axis_index("req")
    row0 = lax.axis_index("row") * rows_here

    copies = []
    for tap in range(9):
        copy = pltpu.make_async_copy(
            mid_w_hbm.at[pl.ds(3 * tap, 3)], mid_w.at[pl.ds(3 * tap, 3)], sems.at[tap]
        )
        copy.start()
        copies.append(copy)

    def keep_of(d):
        start = jnp.int32(0)
        first = d <= 0
        for r in range(counts_ref.shape[0]):
            first = jnp.logical_or(first, start == d)
            start = start + counts_ref[r]
        return jnp.where(first, 0.0, 1.0).astype(jnp.float32)

    keep_own = keep_of(me)
    keep_prev = keep_of(me - 1)

    half = LANES // 2
    three = 3 * C_LAT
    in_w[...] = jnp.zeros_like(in_w)
    for t in range(3):
        for i in range(3):
            if i < 2:
                base = t * LANES + i * half
            else:
                base = 3 * LANES + t * half
            in_w[base : base + three, :] = in_w_ref[(3 * t + i) * three : (3 * t + i + 1) * three, :]

    zero_slab = jnp.zeros((width, LANES), jnp.bfloat16)
    for f in range(frames_in):
        pair_rows[f, 0] = zero_slab
    for f in range(frames_in + 1):
        pair_time[f, height] = zero_slab
    for y in range(height):
        pair_time[frames_in, y] = zero_slab

    place = lax.broadcasted_iota(jnp.int32, (width, LANES), 0) % 8
    lane = lax.broadcasted_iota(jnp.int32, (width, LANES), 1)
    low = jnp.logical_and(place == 0, lane < C_LAT)
    high = jnp.logical_and(place == 7, jnp.logical_and(lane >= 2 * C_LAT, lane < three))
    bits = [lax.rem(place // (1 << n), 2) == 1 for n in range(3)]
    edge = jnp.zeros((8, LANES), jnp.float32)

    def place_row(f, y, line):
        spread = jnp.concatenate(
            [
                jnp.broadcast_to(line[:, LANES * b : LANES * (b + 1)], (8, LANES))
                for b in range(blocks)
            ],
            axis=0,
        )
        turned = jnp.where(bits[0], spread, pltpu.roll(spread, C_LAT, 1))
        turned = jnp.where(bits[1], pltpu.roll(turned, LANES - 2 * C_LAT, 1), turned)
        turned = jnp.where(bits[2], pltpu.roll(turned, LANES - 4 * C_LAT, 1), turned)
        before = jnp.concatenate([edge, turned[:-8]], axis=0)
        after = jnp.concatenate([turned[8:], edge], axis=0)
        window = jnp.where(low, before, jnp.where(high, after, turned))
        other = pltpu.roll(window, half, 1).astype(jnp.bfloat16)
        window = window.astype(jnp.bfloat16)
        pair_rows[f, y + 1, :, :half] = window[:, :half]
        pair_rows[f, y, :, half:] = other[:, half:]
        pair_time[f + 1, y, :, :half] = window[:, :half]
        pair_time[f, y, :, half:] = other[:, half:]

    @pl.loop(0, frames_in)
    def _(f):
        keep = jnp.where(f < CF, keep_prev, jnp.where(f < 2 * CF, keep_own, 1.0))

        @pl.loop(0, row_n)
        def _(r):
            shards = [x_ref[r, q, f // CF, f % CF].astype(jnp.float32) for q in range(req_n)]
            merged = jnp.concatenate(shards, axis=1) * keep
            for here in range(rows_here):
                place_row(f, r * rows_here + here, merged[here : here + 1])

    sums = []
    cells = height * width
    for f in range(outs):
        taps = [
            pair_rows[f, :height],
            pair_rows[f + 1, :height],
            pair_rows[f + 2, :height],
            pair_time[f + 1, 1:],
            pair_time[f + 3, 1:],
        ]
        stacked = jnp.concatenate([tap.reshape(cells, LANES) for tap in taps], axis=1)
        hidden = jnp.dot(stacked, in_w[...], preferred_element_type=jnp.float32) + in_b
        hid[f] = hidden.reshape(height, width, chans)
        sums.append(jnp.sum(hidden, axis=0, keepdims=True))
        sums.append(jnp.sum(hidden * hidden, axis=0, keepdims=True))
    per_group = chans // G
    down = lax.broadcasted_iota(jnp.int32, (chans, chans), 0) // per_group
    over = lax.broadcasted_iota(jnp.int32, (chans, chans), 1) // per_group
    same = jnp.where(down == over, 1.0, 0.0).astype(jnp.float32)
    grouped = jnp.dot(
        jnp.concatenate(sums, axis=0),
        same,
        precision=lax.Precision.HIGHEST,
        preferred_element_type=jnp.float32,
    ) / (cells * per_group)

    span_rows = rows_here + 2
    for f in range(outs):
        mean = grouped[2 * f : 2 * f + 1]
        var = grouped[2 * f + 1 : 2 * f + 2] - mean * mean
        scale = lax.rsqrt(var + 1e-06) * gain

        @pl.loop(0, span_rows)
        def _(y, f=f, mean=mean, scale=scale):
            row = row0 + y - 1
            inside = jnp.logical_and(row >= 0, row < height)
            value = hid[f, jnp.clip(row, 0, height - 1)]
            value = (value - mean) * scale + nbias
            keep = jnp.where(inside, keep_own if f < CF else 1.0, 0.0)
            value = 0.5 * value * (1.0 + jnp.tanh(0.5 * value)) * keep
            nil = jnp.zeros((1, chans), jnp.float32)
            left = jnp.concatenate([nil, value[:-1]], axis=0)
            right = jnp.concatenate([value[1:], nil], axis=0)
            act[f, y, :, :chans] = left.astype(jnp.bfloat16)
            act[f, y, :, chans : 2 * chans] = value.astype(jnp.bfloat16)
            act[f, y, :, 2 * chans :] = right.astype(jnp.bfloat16)

    many = CF * rows_here * width
    total = hid[pl.ds(outs - CF, CF), pl.ds(row0, rows_here)].reshape(many, chans) + mid_b
    for t in range(3):
        for i in range(3):
            tap = 3 * t + i
            copies[tap].wait()
            cells_in = act[t : t + CF, i : i + rows_here].reshape(many, 3 * chans)
            weight = mid_w[3 * tap : 3 * tap + 3].reshape(3 * chans, chans)
            total = total + jnp.dot(cells_in, weight, preferred_element_type=jnp.float32)
    out_ref[...] = total.astype(jnp.bfloat16).reshape(CF, rows_here, width, chans)


def decode(counts, frames, rows_here, in_weight, in_bias, norm_gain, norm_bias, mid_weight, mid_bias):
    frames_in = DEPTH * CF
    height = frames.shape[0] * rows_here
    chans = in_weight.shape[1]
    outs = frames_in - 2
    vmem = pl.BlockSpec(memory_space=pltpu.VMEM)
    return pl.pallas_call(
        functools.partial(decode_kernel, rows_here),
        out_shape=jax.ShapeDtypeStruct((CF, rows_here, W, chans), jnp.bfloat16),
        in_specs=[pl.BlockSpec(memory_space=pltpu.SMEM)] + [vmem] * 6 + [pl.BlockSpec(memory_space=pl.ANY)],
        out_specs=vmem,
        scratch_shapes=[
            pltpu.VMEM(mid_weight.shape, jnp.bfloat16),
            pltpu.VMEM((5 * LANES, chans), jnp.bfloat16),
            pltpu.VMEM((frames_in, height + 1, W, LANES), jnp.bfloat16),
            pltpu.VMEM((frames_in + 1, height + 1, W, LANES), jnp.bfloat16),
            pltpu.VMEM((outs, height, W, chans), jnp.float32),
            pltpu.VMEM((outs, rows_here + 2, W, 3 * chans), jnp.bfloat16),
            pltpu.SemaphoreType.DMA((9,)),
        ],
        compiler_params=pltpu.CompilerParams(vmem_limit_bytes=58 * 1024 * 1024),
        name="span_decode",
    )(
        counts,
        frames,
        in_weight,
        in_bias,
        norm_gain,
        norm_bias,
        mid_bias,
        mid_weight,
    )


def local(
    latents,
    dispatch_plan,
    span_counts,
    in_weight,
    in_bias,
    norm_gain,
    norm_bias,
    mid_weight,
    mid_bias,
):
    rows_here = latents.shape[2]
    chans = mid_weight.shape[2]
    arrived = exchange(latents, dispatch_plan)
    mixed = decode(
        span_counts, arrived, rows_here, in_weight, in_bias, norm_gain, norm_bias, mid_weight, mid_bias
    )
    return mixed.reshape(1, CF, rows_here, W * chans)


def solution(mesh):
    placed = (
        P("groups", None, "row", "req"),
        P("groups"),
        P("groups"),
        P(),
        P(),
        P(),
        P(),
        P(),
        P(),
    )
    return jax.shard_map(
        local,
        mesh=mesh,
        in_specs=placed,
        out_specs=P(("groups", "req"), None, "row", None),
        check_vma=False,
    )
```

```python
import functools

import jax
import jax.numpy as jnp
from jax import lax
from jax.experimental import pallas as pl
from jax.experimental.pallas import tpu as pltpu
from jax.sharding import PartitionSpec as P

C_LAT = 16
G = 32
CF = 2
W = 160
LANES = 128
DEPTH = 3
MESH = pl.DeviceIdType.MESH


def span_kernel(
    req_n,
    row_n,
    lat_hbm,
    plan_hbm,
    counts_hbm,
    in_w_hbm,
    in_b_hbm,
    gain_hbm,
    nbias_hbm,
    mid_w_hbm,
    mid_b_hbm,
    out_ref,
    lat_ref,
    plan_ref,
    counts_ref,
    in_w_ref,
    in_b_ref,
    gain_ref,
    nbias_ref,
    mid_b_ref,
    sel,
    x_ref,
    mid_w,
    in_w,
    pair_rows,
    pair_time,
    hid,
    act,
    sems,
    send_sems,
    recv_sems,
):
    me = lax.axis_index("req")
    me_row = lax.axis_index("row")
    devices = req_n * row_n
    flat = me_row * req_n + me
    rows_here = lat_ref.shape[2]
    row0 = me_row * rows_here

    def peer(k):
        target = lax.rem(flat + k, devices)
        return {"row": target // req_n, "req": lax.rem(target, req_n)}

    barrier = pltpu.get_barrier_semaphore()
    for k in range(1, devices):
        pl.semaphore_signal(barrier, inc=1, device_id=peer(k), device_id_type=MESH)
    loads = [
        pltpu.make_async_copy(source, target, sems.at[9 + n])
        for n, (source, target) in enumerate(
            (
                (plan_hbm, plan_ref),
                (lat_hbm, lat_ref),
                (counts_hbm, counts_ref),
                (in_w_hbm, in_w_ref),
                (in_b_hbm, in_b_ref),
                (gain_hbm, gain_ref),
                (nbias_hbm, nbias_ref),
                (mid_b_hbm, mid_b_ref),
            )
        )
    ]
    for load in loads:
        load.start()
    copies = []
    for tap in range(9):
        copy = pltpu.make_async_copy(
            mid_w_hbm.at[pl.ds(3 * tap, 3)], mid_w.at[pl.ds(3 * tap, 3)], sems.at[tap]
        )
        copy.start()
        copies.append(copy)
    loads[0].wait()
    loads[1].wait()
    for d in range(DEPTH - 1):
        sel[d] = jnp.zeros_like(sel[d])
    for d in range(req_n):
        sel[d + DEPTH - 1] = lat_ref[plan_ref[d]]
    pl.semaphore_wait(barrier, devices - 1)
    sends = []
    for k in range(1, devices):
        where = peer(k)
        send = pltpu.make_async_remote_copy(
            src_ref=sel.at[pl.ds(where["req"], DEPTH)],
            dst_ref=x_ref.at[me_row, me],
            send_sem=send_sems.at[k],
            recv_sem=recv_sems.at[k],
            device_id=where,
            device_id_type=MESH,
        )
        send.start()
        sends.append(send)
    x_ref[me_row, me] = sel[pl.ds(me, DEPTH)]
    for load in loads[2:]:
        load.wait()

    frames_in = DEPTH * CF
    height = row_n * rows_here
    width = req_n * x_ref.shape[5] // C_LAT
    blocks = width * C_LAT // LANES
    chans = in_w_ref.shape[1]
    outs = frames_in - 2
    in_b = in_b_ref[...].reshape(1, chans)
    gain = gain_ref[...].reshape(1, chans)
    nbias = nbias_ref[...].reshape(1, chans)
    mid_b = mid_b_ref[...].reshape(1, chans)
    def keep_of(d):
        start = jnp.int32(0)
        first = d <= 0
        for r in range(counts_ref.shape[0]):
            first = jnp.logical_or(first, start == d)
            start = start + counts_ref[r]
        return jnp.where(first, 0.0, 1.0).astype(jnp.float32)

    keep_own = keep_of(me)
    keep_prev = keep_of(me - 1)

    half = LANES // 2
    three = 3 * C_LAT
    in_w[...] = jnp.zeros_like(in_w)
    for t in range(3):
        for i in range(3):
            if i < 2:
                base = t * LANES + i * half
            else:
                base = 3 * LANES + t * half
            in_w[base : base + three, :] = in_w_ref[(3 * t + i) * three : (3 * t + i + 1) * three, :]

    zero_slab = jnp.zeros((width, LANES), jnp.bfloat16)
    for f in range(frames_in):
        pair_rows[f, 0] = zero_slab
    for f in range(frames_in + 1):
        pair_time[f, height] = zero_slab
    for y in range(height):
        pair_time[frames_in, y] = zero_slab

    place = lax.broadcasted_iota(jnp.int32, (width, LANES), 0) % 8
    lane = lax.broadcasted_iota(jnp.int32, (width, LANES), 1)
    low = jnp.logical_and(place == 0, lane < C_LAT)
    high = jnp.logical_and(place == 7, jnp.logical_and(lane >= 2 * C_LAT, lane < three))
    bits = [lax.rem(place // (1 << n), 2) == 1 for n in range(3)]
    edge = jnp.zeros((8, LANES), jnp.float32)

    def place_row(f, y, line):
        spread = jnp.concatenate(
            [
                jnp.broadcast_to(line[:, LANES * b : LANES * (b + 1)], (8, LANES))
                for b in range(blocks)
            ],
            axis=0,
        )
        turned = jnp.where(bits[0], spread, pltpu.roll(spread, C_LAT, 1))
        turned = jnp.where(bits[1], pltpu.roll(turned, LANES - 2 * C_LAT, 1), turned)
        turned = jnp.where(bits[2], pltpu.roll(turned, LANES - 4 * C_LAT, 1), turned)
        before = jnp.concatenate([edge, turned[:-8]], axis=0)
        after = jnp.concatenate([turned[8:], edge], axis=0)
        window = jnp.where(low, before, jnp.where(high, after, turned))
        other = pltpu.roll(window, half, 1).astype(jnp.bfloat16)
        window = window.astype(jnp.bfloat16)
        pair_rows[f, y + 1, :, :half] = window[:, :half]
        pair_rows[f, y, :, half:] = other[:, half:]
        pair_time[f + 1, y, :, :half] = window[:, :half]
        pair_time[f, y, :, half:] = other[:, half:]

    for send in sends:
        send.wait()

    @pl.loop(0, frames_in)
    def _(f):
        keep = jnp.where(f < CF, keep_prev, jnp.where(f < 2 * CF, keep_own, 1.0))

        @pl.loop(0, row_n)
        def _(r):
            shards = [x_ref[r, q, f // CF, f % CF].astype(jnp.float32) for q in range(req_n)]
            merged = jnp.concatenate(shards, axis=1) * keep
            for here in range(rows_here):
                place_row(f, r * rows_here + here, merged[here : here + 1])

    sums = []
    cells = height * width
    for f in range(outs):
        taps = [
            pair_rows[f, :height],
            pair_rows[f + 1, :height],
            pair_rows[f + 2, :height],
            pair_time[f + 1, 1:],
            pair_time[f + 3, 1:],
        ]
        stacked = jnp.concatenate([tap.reshape(cells, LANES) for tap in taps], axis=1)
        hidden = jnp.dot(stacked, in_w[...], preferred_element_type=jnp.float32) + in_b
        hid[f] = hidden.reshape(height, width, chans)
        sums.append(jnp.sum(hidden, axis=0, keepdims=True))
        sums.append(jnp.sum(hidden * hidden, axis=0, keepdims=True))
    per_group = chans // G
    down = lax.broadcasted_iota(jnp.int32, (chans, chans), 0) // per_group
    over = lax.broadcasted_iota(jnp.int32, (chans, chans), 1) // per_group
    same = jnp.where(down == over, 1.0, 0.0).astype(jnp.float32)
    grouped = jnp.dot(
        jnp.concatenate(sums, axis=0),
        same,
        precision=lax.Precision.HIGHEST,
        preferred_element_type=jnp.float32,
    ) / (cells * per_group)

    span_rows = rows_here + 2
    for f in range(outs):
        mean = grouped[2 * f : 2 * f + 1]
        var = grouped[2 * f + 1 : 2 * f + 2] - mean * mean
        scale = lax.rsqrt(var + 1e-06) * gain

        @pl.loop(0, span_rows)
        def _(y, f=f, mean=mean, scale=scale):
            row = row0 + y - 1
            inside = jnp.logical_and(row >= 0, row < height)
            value = hid[f, jnp.clip(row, 0, height - 1)]
            value = (value - mean) * scale + nbias
            keep = jnp.where(inside, keep_own if f < CF else 1.0, 0.0)
            value = 0.5 * value * (1.0 + jnp.tanh(0.5 * value)) * keep
            act[f, y] = value.astype(jnp.bfloat16)

    many = CF * rows_here * width
    for copy in copies:
        copy.wait()
    slabs = []
    weights = []
    for t in range(3):
        for i in range(3):
            tap = 3 * (3 * t + i)
            slabs.append(act[t : t + CF, i : i + rows_here].reshape(many, chans))
            weights.append(jnp.concatenate([mid_w[tap + j] for j in range(3)], axis=1))
    columns = jnp.dot(
        jnp.concatenate(slabs, axis=1),
        jnp.concatenate(weights, axis=0),
        preferred_element_type=jnp.float32,
    ).reshape(CF * rows_here, width, 3 * chans)
    nil = jnp.zeros((1, chans), jnp.float32)
    for f in range(CF):
        for y in range(rows_here):
            part = columns[f * rows_here + y]
            total = hid[outs - CF + f, row0 + y] + mid_b + part[:, chans : 2 * chans]
            total = total + jnp.concatenate([nil, part[:-1, :chans]], axis=0)
            total = total + jnp.concatenate([part[1:, 2 * chans :], nil], axis=0)
            out_ref[f, y] = total.astype(jnp.bfloat16)


def spans(latents, dispatch_plan, span_counts, in_weight, in_bias, norm_gain, norm_bias, mid_weight, mid_bias):
    req_n = lax.axis_size("req")
    row_n = lax.axis_size("row")
    frames, rows_here, lanes = latents.shape[1:]
    chans = in_weight.shape[1]
    frames_in = DEPTH * CF
    outs = frames_in - 2
    height = row_n * rows_here
    return pl.pallas_call(
        functools.partial(span_kernel, req_n, row_n),
        out_shape=jax.ShapeDtypeStruct((CF, rows_here, W, chans), jnp.bfloat16),
        in_specs=[pl.BlockSpec(memory_space=pl.ANY)] * 9,
        out_specs=pl.BlockSpec(memory_space=pltpu.VMEM),
        scratch_shapes=[
            pltpu.VMEM(latents.shape, latents.dtype),
            pltpu.SMEM(dispatch_plan.shape, jnp.int32),
            pltpu.SMEM(span_counts.shape, jnp.int32),
            pltpu.VMEM(in_weight.shape, in_weight.dtype),
            pltpu.VMEM((chans,), jnp.float32),
            pltpu.VMEM((chans,), jnp.float32),
            pltpu.VMEM((chans,), jnp.float32),
            pltpu.VMEM((chans,), jnp.float32),
            pltpu.VMEM((req_n + DEPTH - 1, frames, rows_here, lanes), latents.dtype),
            pltpu.VMEM((row_n, req_n, DEPTH, frames, rows_here, lanes), latents.dtype),
            pltpu.VMEM(mid_weight.shape, jnp.bfloat16),
            pltpu.VMEM((5 * LANES, chans), jnp.bfloat16),
            pltpu.VMEM((frames_in, height + 1, W, LANES), jnp.bfloat16),
            pltpu.VMEM((frames_in + 1, height + 1, W, LANES), jnp.bfloat16),
            pltpu.VMEM((outs, height, W, chans), jnp.float32),
            pltpu.VMEM((outs, rows_here + 2, W, chans), jnp.bfloat16),
            pltpu.SemaphoreType.DMA((17,)),
            pltpu.SemaphoreType.DMA((req_n * row_n,)),
            pltpu.SemaphoreType.DMA((req_n * row_n,)),
        ],
        compiler_params=pltpu.CompilerParams(
            collective_id=0, has_side_effects=True, vmem_limit_bytes=58 * 1024 * 1024
        ),
        name="spans",
    )(
        latents,
        dispatch_plan,
        span_counts,
        in_weight,
        in_bias,
        norm_gain,
        norm_bias,
        mid_weight,
        mid_bias,
    )


def local(
    latents,
    dispatch_plan,
    span_counts,
    in_weight,
    in_bias,
    norm_gain,
    norm_bias,
    mid_weight,
    mid_bias,
):
    rows_here = latents.shape[2]
    chans = mid_weight.shape[2]
    mixed = spans(
        latents,
        dispatch_plan,
        span_counts,
        in_weight,
        in_bias,
        norm_gain,
        norm_bias,
        mid_weight,
        mid_bias,
    )
    return mixed.reshape(1, CF, rows_here, W * chans)


def solution(mesh):
    placed = (
        P("groups", None, "row", "req"),
        P("groups"),
        P("groups"),
        P(),
        P(),
        P(),
        P(),
        P(),
        P(),
    )
    return jax.shard_map(
        local,
        mesh=mesh,
        in_specs=placed,
        out_specs=P(("groups", "req"), None, "row", None),
        check_vma=False,
    )
```

```python
import functools

import jax
import jax.numpy as jnp
from jax import lax
from jax.experimental import pallas as pl
from jax.experimental.pallas import tpu as pltpu
from jax.sharding import PartitionSpec as P

C_LAT = 16
G = 32
CF = 2
W = 160
LANES = 128
DEPTH = 3
MESH = pl.DeviceIdType.MESH


def span_kernel(
    req_n,
    row_n,
    lat_hbm,
    plan_hbm,
    counts_hbm,
    in_w_hbm,
    in_b_hbm,
    gain_hbm,
    nbias_hbm,
    mid_w_hbm,
    mid_b_hbm,
    out_ref,
    lat_ref,
    plan_ref,
    counts_ref,
    in_w_ref,
    in_b_ref,
    gain_ref,
    nbias_ref,
    mid_b_ref,
    sel,
    x_ref,
    mid_w,
    in_w,
    pair_rows,
    pair_time,
    hid,
    act,
    lines,
    fanned,
    sems,
    send_sems,
    recv_sems,
):
    me = lax.axis_index("req")
    me_row = lax.axis_index("row")
    devices = req_n * row_n
    flat = me_row * req_n + me
    rows_here = lat_ref.shape[2]
    row0 = me_row * rows_here

    def peer(k):
        target = lax.rem(flat + k, devices)
        return {"row": target // req_n, "req": lax.rem(target, req_n)}

    barrier = pltpu.get_barrier_semaphore()
    for k in range(1, devices):
        pl.semaphore_signal(barrier, inc=1, device_id=peer(k), device_id_type=MESH)
    loads = [
        pltpu.make_async_copy(source, target, sems.at[9 + n])
        for n, (source, target) in enumerate(
            (
                (plan_hbm, plan_ref),
                (lat_hbm, lat_ref),
                (counts_hbm, counts_ref),
                (in_w_hbm, in_w_ref),
                (in_b_hbm, in_b_ref),
                (gain_hbm, gain_ref),
                (nbias_hbm, nbias_ref),
                (mid_b_hbm, mid_b_ref),
            )
        )
    ]
    for load in loads:
        load.start()
    copies = []
    for tap in range(9):
        copy = pltpu.make_async_copy(
            mid_w_hbm.at[pl.ds(3 * tap, 3)], mid_w.at[pl.ds(3 * tap, 3)], sems.at[tap]
        )
        copy.start()
        copies.append(copy)
    loads[0].wait()
    loads[1].wait()
    for d in range(DEPTH - 1):
        sel[d] = jnp.zeros_like(sel[d])
    for d in range(req_n):
        span = lat_ref[plan_ref[d]].astype(jnp.float32)
        sel[d + DEPTH - 1] = jnp.concatenate([span[f] for f in range(CF)], axis=1).astype(sel.dtype)
    pl.semaphore_wait(barrier, devices - 1)
    sends = []
    for k in range(1, devices):
        where = peer(k)
        send = pltpu.make_async_remote_copy(
            src_ref=sel.at[pl.ds(where["req"], DEPTH)],
            dst_ref=x_ref.at[me_row, me],
            send_sem=send_sems.at[k],
            recv_sem=recv_sems.at[k],
            device_id=where,
            device_id_type=MESH,
        )
        send.start()
        sends.append(send)
    x_ref[me_row, me] = sel[pl.ds(me, DEPTH)]
    for load in loads[2:]:
        load.wait()

    frames_in = DEPTH * CF
    height = row_n * rows_here
    lanes = x_ref.shape[4] // CF
    width = req_n * lanes // C_LAT
    blocks = width * C_LAT // LANES
    chans = in_w_ref.shape[1]
    outs = frames_in - 2
    in_b = in_b_ref[...].reshape(1, chans)
    gain = gain_ref[...].reshape(1, chans)
    nbias = nbias_ref[...].reshape(1, chans)
    mid_b = mid_b_ref[...].reshape(1, chans)
    def keep_of(d):
        start = jnp.int32(0)
        first = d <= 0
        for r in range(counts_ref.shape[0]):
            first = jnp.logical_or(first, start == d)
            start = start + counts_ref[r]
        return jnp.where(first, 0.0, 1.0).astype(jnp.float32)

    keep_own = keep_of(me)
    keep_prev = keep_of(me - 1)

    half = LANES // 2
    three = 3 * C_LAT
    in_w[...] = jnp.zeros_like(in_w)
    for t in range(3):
        for i in range(3):
            if i < 2:
                base = t * LANES + i * half
            else:
                base = 3 * LANES + t * half
            in_w[base : base + three, :] = in_w_ref[(3 * t + i) * three : (3 * t + i + 1) * three, :]

    zero_slab = jnp.zeros((width, LANES), jnp.bfloat16)
    for f in range(frames_in):
        pair_rows[f, 0] = zero_slab
    for f in range(frames_in + 1):
        pair_time[f, height] = zero_slab
    for y in range(height):
        pair_time[frames_in, y] = zero_slab

    lane = lax.broadcasted_iota(jnp.int32, (blocks, LANES), 1)
    low = lane < C_LAT
    high = jnp.logical_and(lane >= 2 * C_LAT, lane < three)
    left = lane < half
    nothing = jnp.zeros((1, LANES), jnp.float32)

    def place_row(f, y, here):
        cells = lines[pl.ds(here, blocks, stride=rows_here), :]
        turned = [pltpu.roll(cells, (C_LAT - C_LAT * p) % LANES, 1) if p != 1 else cells for p in range(8)]
        for p in range(8):
            window = turned[p]
            other = turned[(p + 4) % 8]
            if p == 0:
                before = jnp.concatenate([nothing, window[:-1]], axis=0)
                window = jnp.where(low, before, window)
                other = pltpu.roll(window, half, 1)
            if p == 7:
                after = jnp.concatenate([window[1:], nothing], axis=0)
                window = jnp.where(high, after, window)
                other = pltpu.roll(window, half, 1)
            fanned[here, pl.ds(p, blocks, stride=8), :] = jnp.where(left, window, other)
        both = fanned[here].astype(jnp.bfloat16)
        pair_rows[f, y + 1, :, :half] = both[:, :half]
        pair_rows[f, y, :, half:] = both[:, half:]
        pair_time[f + 1, y, :, :half] = both[:, :half]
        pair_time[f, y, :, half:] = both[:, half:]

    for send in sends:
        send.wait()

    @pl.loop(0, DEPTH)
    def _(span):
        keep = jnp.where(span == 0, keep_prev, jnp.where(span == 1, keep_own, 1.0))

        @pl.loop(0, row_n)
        def _(r):
            shards = [x_ref[r, q, span].astype(jnp.float32) * keep for q in range(req_n)]
            for frame in range(CF):
                merged = jnp.concatenate(
                    [shard[:, frame * lanes : (frame + 1) * lanes] for shard in shards], axis=1
                )
                for b in range(blocks):
                    lines[b * rows_here : (b + 1) * rows_here, :] = merged[:, b * LANES : (b + 1) * LANES]
                for here in range(rows_here):
                    place_row(span * CF + frame, r * rows_here + here, here)

    sums = []
    cells = height * width
    for f in range(outs):
        taps = [
            pair_rows[f, :height],
            pair_rows[f + 1, :height],
            pair_rows[f + 2, :height],
            pair_time[f + 1, 1:],
            pair_time[f + 3, 1:],
        ]
        stacked = jnp.concatenate([tap.reshape(cells, LANES) for tap in taps], axis=1)
        hidden = jnp.dot(stacked, in_w[...], preferred_element_type=jnp.float32) + in_b
        hid[f] = hidden.reshape(height, width, chans)
        sums.append(jnp.sum(hidden, axis=0, keepdims=True))
        sums.append(jnp.sum(hidden * hidden, axis=0, keepdims=True))
    per_group = chans // G
    down = lax.broadcasted_iota(jnp.int32, (chans, chans), 0) // per_group
    over = lax.broadcasted_iota(jnp.int32, (chans, chans), 1) // per_group
    same = jnp.where(down == over, 1.0, 0.0).astype(jnp.float32)
    grouped = jnp.dot(
        jnp.concatenate(sums, axis=0),
        same,
        precision=lax.Precision.HIGHEST,
        preferred_element_type=jnp.float32,
    ) / (cells * per_group)

    span_rows = rows_here + 2
    for f in range(outs):
        mean = grouped[2 * f : 2 * f + 1]
        var = grouped[2 * f + 1 : 2 * f + 2] - mean * mean
        scale = lax.rsqrt(var + 1e-06) * gain

        @pl.loop(0, span_rows)
        def _(y, f=f, mean=mean, scale=scale):
            row = row0 + y - 1
            inside = jnp.logical_and(row >= 0, row < height)
            @pl.when(inside)
            def _():
                value = (hid[f, row] - mean) * scale + nbias
                value = 0.5 * value * (1.0 + jnp.tanh(0.5 * value))
                if f < CF:
                    value = value * keep_own
                act[f, y] = value.astype(jnp.bfloat16)

            @pl.when(jnp.logical_not(inside))
            def _():
                act[f, y] = jnp.zeros((width, chans), jnp.bfloat16)

    many = CF * rows_here * width
    for copy in copies:
        copy.wait()
    slabs = []
    weights = []
    for t in range(3):
        for i in range(3):
            tap = 3 * (3 * t + i)
            slabs.append(act[t : t + CF, i : i + rows_here].reshape(many, chans))
            weights.append(jnp.concatenate([mid_w[tap + j] for j in range(3)], axis=1))
    columns = jnp.dot(
        jnp.concatenate(slabs, axis=1),
        jnp.concatenate(weights, axis=0),
        preferred_element_type=jnp.float32,
    ).reshape(CF * rows_here, width, 3 * chans)
    nil = jnp.zeros((1, chans), jnp.float32)
    for f in range(CF):
        for y in range(rows_here):
            part = columns[f * rows_here + y]
            total = hid[outs - CF + f, row0 + y] + mid_b + part[:, chans : 2 * chans]
            total = total + jnp.concatenate([nil, part[:-1, :chans]], axis=0)
            total = total + jnp.concatenate([part[1:, 2 * chans :], nil], axis=0)
            out_ref[f, y] = total.astype(jnp.bfloat16)


def spans(latents, dispatch_plan, span_counts, in_weight, in_bias, norm_gain, norm_bias, mid_weight, mid_bias):
    req_n = lax.axis_size("req")
    row_n = lax.axis_size("row")
    frames, rows_here, lanes = latents.shape[1:]
    chans = in_weight.shape[1]
    frames_in = DEPTH * CF
    outs = frames_in - 2
    height = row_n * rows_here
    blocks = W * C_LAT // LANES
    return pl.pallas_call(
        functools.partial(span_kernel, req_n, row_n),
        out_shape=jax.ShapeDtypeStruct((CF, rows_here, W, chans), jnp.bfloat16),
        in_specs=[pl.BlockSpec(memory_space=pl.ANY)] * 9,
        out_specs=pl.BlockSpec(memory_space=pltpu.VMEM),
        scratch_shapes=[
            pltpu.VMEM(latents.shape, latents.dtype),
            pltpu.SMEM(dispatch_plan.shape, jnp.int32),
            pltpu.SMEM(span_counts.shape, jnp.int32),
            pltpu.VMEM(in_weight.shape, in_weight.dtype),
            pltpu.VMEM((chans,), jnp.float32),
            pltpu.VMEM((chans,), jnp.float32),
            pltpu.VMEM((chans,), jnp.float32),
            pltpu.VMEM((chans,), jnp.float32),
            pltpu.VMEM((req_n + DEPTH - 1, rows_here, frames * lanes), latents.dtype),
            pltpu.VMEM((row_n, req_n, DEPTH, rows_here, frames * lanes), latents.dtype),
            pltpu.VMEM(mid_weight.shape, jnp.bfloat16),
            pltpu.VMEM((5 * LANES, chans), jnp.bfloat16),
            pltpu.VMEM((frames_in, height + 1, W, LANES), jnp.bfloat16),
            pltpu.VMEM((frames_in + 1, height + 1, W, LANES), jnp.bfloat16),
            pltpu.VMEM((outs, height, W, chans), jnp.float32),
            pltpu.VMEM((outs, rows_here + 2, W, chans), jnp.bfloat16),
            pltpu.VMEM((blocks * rows_here, LANES), jnp.float32),
            pltpu.VMEM((rows_here, W, LANES), jnp.float32),
            pltpu.SemaphoreType.DMA((17,)),
            pltpu.SemaphoreType.DMA((req_n * row_n,)),
            pltpu.SemaphoreType.DMA((req_n * row_n,)),
        ],
        compiler_params=pltpu.CompilerParams(
            collective_id=0, has_side_effects=True, vmem_limit_bytes=58 << 20
        ),
        name="spans",
    )(
        latents,
        dispatch_plan,
        span_counts,
        in_weight,
        in_bias,
        norm_gain,
        norm_bias,
        mid_weight,
        mid_bias,
    )


def local(
    latents,
    dispatch_plan,
    span_counts,
    in_weight,
    in_bias,
    norm_gain,
    norm_bias,
    mid_weight,
    mid_bias,
):
    rows_here = latents.shape[2]
    chans = mid_weight.shape[2]
    mixed = spans(
        latents,
        dispatch_plan,
        span_counts,
        in_weight,
        in_bias,
        norm_gain,
        norm_bias,
        mid_weight,
        mid_bias,
    )
    return mixed.reshape(1, CF, rows_here, W * chans)


def solution(mesh):
    placed = (
        P("groups", None, "row", "req"),
        P("groups"),
        P("groups"),
        P(),
        P(),
        P(),
        P(),
        P(),
        P(),
    )
    return jax.shard_map(
        local,
        mesh=mesh,
        in_specs=placed,
        out_specs=P(("groups", "req"), None, "row", None),
        check_vma=False,
    )
```

```python
import functools

import jax
import jax.numpy as jnp
from jax import lax
from jax.experimental import pallas as pl
from jax.experimental.pallas import tpu as pltpu
from jax.sharding import PartitionSpec as P

C_LAT = 16
G = 32
CF = 2
W = 160
LANES = 128
DEPTH = 3
MESH = pl.DeviceIdType.MESH


def span_kernel(
    req_n,
    row_n,
    lat_hbm,
    plan_hbm,
    counts_hbm,
    in_w_hbm,
    in_b_hbm,
    gain_hbm,
    nbias_hbm,
    mid_w_hbm,
    mid_b_hbm,
    out_ref,
    lat_ref,
    plan_ref,
    counts_ref,
    in_w_ref,
    in_b_ref,
    gain_ref,
    nbias_ref,
    mid_b_ref,
    sel,
    x_ref,
    mid_w,
    in_w,
    pair_rows,
    pair_time,
    hid,
    act,
    lines,
    fanned,
    sems,
    send_sems,
    recv_sems,
):
    me = lax.axis_index("req")
    me_row = lax.axis_index("row")
    devices = req_n * row_n
    flat = me_row * req_n + me
    rows_here = lat_ref.shape[2]
    row0 = me_row * rows_here

    def peer(k):
        target = lax.rem(flat + k, devices)
        return {"row": target // req_n, "req": lax.rem(target, req_n)}

    barrier = pltpu.get_barrier_semaphore()
    for k in range(1, devices):
        pl.semaphore_signal(barrier, inc=1, device_id=peer(k), device_id_type=MESH)
    loads = [
        pltpu.make_async_copy(source, target, sems.at[9 + n])
        for n, (source, target) in enumerate(
            (
                (plan_hbm, plan_ref),
                (lat_hbm, lat_ref),
                (counts_hbm, counts_ref),
                (in_w_hbm, in_w_ref),
                (in_b_hbm, in_b_ref),
                (gain_hbm, gain_ref),
                (nbias_hbm, nbias_ref),
                (mid_b_hbm, mid_b_ref),
            )
        )
    ]
    for load in loads:
        load.start()
    copies = []
    for tap in range(9):
        copy = pltpu.make_async_copy(
            mid_w_hbm.at[pl.ds(3 * tap, 3)], mid_w.at[pl.ds(3 * tap, 3)], sems.at[tap]
        )
        copy.start()
        copies.append(copy)
    loads[0].wait()
    loads[1].wait()
    for d in range(DEPTH - 1):
        sel[d] = jnp.zeros_like(sel[d])
    for d in range(req_n):
        span = lat_ref[plan_ref[d]].astype(jnp.float32)
        sel[d + DEPTH - 1] = jnp.concatenate([span[f] for f in range(CF)], axis=1).astype(sel.dtype)
    pl.semaphore_wait(barrier, devices - 1)
    sends = []
    for k in range(1, devices):
        where = peer(k)
        send = pltpu.make_async_remote_copy(
            src_ref=sel.at[pl.ds(where["req"], DEPTH)],
            dst_ref=x_ref.at[me_row, me],
            send_sem=send_sems.at[k],
            recv_sem=recv_sems.at[k],
            device_id=where,
            device_id_type=MESH,
        )
        send.start()
        sends.append(send)
    x_ref[me_row, me] = sel[pl.ds(me, DEPTH)]
    for load in loads[2:]:
        load.wait()

    frames_in = DEPTH * CF
    height = row_n * rows_here
    lanes = x_ref.shape[4] // CF
    width = req_n * lanes // C_LAT
    blocks = width * C_LAT // LANES
    chans = in_w_ref.shape[1]
    outs = frames_in - 2
    in_b = in_b_ref[...].reshape(1, chans)
    gain = gain_ref[...].reshape(1, chans)
    nbias = nbias_ref[...].reshape(1, chans)
    mid_b = mid_b_ref[...].reshape(1, chans)
    def keep_of(d):
        start = jnp.int32(0)
        first = d <= 0
        for r in range(counts_ref.shape[0]):
            first = jnp.logical_or(first, start == d)
            start = start + counts_ref[r]
        return jnp.where(first, 0.0, 1.0).astype(jnp.float32)

    keep_own = keep_of(me)
    keep_prev = keep_of(me - 1)

    half = LANES // 2
    three = 3 * C_LAT
    in_w[...] = jnp.zeros_like(in_w)
    for t in range(3):
        for i in range(3):
            if i < 2:
                base = t * LANES + i * half
            else:
                base = 3 * LANES + t * half
            in_w[base : base + three, :] = in_w_ref[(3 * t + i) * three : (3 * t + i + 1) * three, :]

    zero_slab = jnp.zeros((width, LANES), jnp.bfloat16)
    for f in range(frames_in):
        pair_rows[f, 0] = zero_slab
    for f in range(frames_in + 1):
        pair_time[f, height] = zero_slab
    for y in range(height):
        pair_time[frames_in, y] = zero_slab

    lane = lax.broadcasted_iota(jnp.int32, (blocks, LANES), 1)
    low = lane < C_LAT
    high = jnp.logical_and(lane >= 2 * C_LAT, lane < three)
    left = lane < half
    nothing = jnp.zeros((1, LANES), jnp.float32)

    def place_row(f, y, here):
        cells = lines[pl.ds(here, blocks, stride=rows_here), :]
        turned = [pltpu.roll(cells, (C_LAT - C_LAT * p) % LANES, 1) if p != 1 else cells for p in range(8)]
        for p in range(8):
            window = turned[p]
            other = turned[(p + 4) % 8]
            if p == 0:
                before = jnp.concatenate([nothing, window[:-1]], axis=0)
                window = jnp.where(low, before, window)
                other = pltpu.roll(window, half, 1)
            if p == 7:
                after = jnp.concatenate([window[1:], nothing], axis=0)
                window = jnp.where(high, after, window)
                other = pltpu.roll(window, half, 1)
            fanned[here, pl.ds(p, blocks, stride=8), :] = jnp.where(left, window, other)
        both = fanned[here].astype(jnp.bfloat16)
        pair_rows[f, y + 1, :, :half] = both[:, :half]
        pair_rows[f, y, :, half:] = both[:, half:]
        pair_time[f + 1, y, :, :half] = both[:, :half]
        pair_time[f, y, :, half:] = both[:, half:]

    for send in sends:
        send.wait()

    @pl.loop(0, DEPTH)
    def _(span):
        keep = jnp.where(span == 0, keep_prev, jnp.where(span == 1, keep_own, 1.0))

        @pl.loop(0, row_n)
        def _(r):
            shards = [x_ref[r, q, span].astype(jnp.float32) * keep for q in range(req_n)]
            for frame in range(CF):
                merged = jnp.concatenate(
                    [shard[:, frame * lanes : (frame + 1) * lanes] for shard in shards], axis=1
                )
                for b in range(blocks):
                    lines[b * rows_here : (b + 1) * rows_here, :] = merged[:, b * LANES : (b + 1) * LANES]
                for here in range(rows_here):
                    place_row(span * CF + frame, r * rows_here + here, here)

    sums = []
    cells = height * width
    for f in range(outs):
        taps = [
            pair_rows[f, :height],
            pair_rows[f + 1, :height],
            pair_rows[f + 2, :height],
            pair_time[f + 1, 1:],
            pair_time[f + 3, 1:],
        ]
        stacked = jnp.concatenate([tap.reshape(cells, LANES) for tap in taps], axis=1)
        hidden = jnp.dot(stacked, in_w[...], preferred_element_type=jnp.float32) + in_b
        hid[f] = hidden.reshape(height, width, chans)
        sums.append(jnp.sum(hidden, axis=0, keepdims=True))
        sums.append(jnp.sum(hidden * hidden, axis=0, keepdims=True))
    per_group = chans // G
    down = lax.broadcasted_iota(jnp.int32, (chans, chans), 0) // per_group
    over = lax.broadcasted_iota(jnp.int32, (chans, chans), 1) // per_group
    same = jnp.where(down == over, 1.0, 0.0).astype(jnp.float32)
    grouped = jnp.dot(
        jnp.concatenate(sums, axis=0),
        same,
        precision=lax.Precision.HIGHEST,
        preferred_element_type=jnp.float32,
    ) / (cells * per_group)

    span_rows = rows_here + 2
    for f in range(outs):
        mean = grouped[2 * f : 2 * f + 1]
        var = grouped[2 * f + 1 : 2 * f + 2] - mean * mean
        scale = lax.rsqrt(var + 1e-06) * gain

        @pl.loop(0, span_rows)
        def _(y, f=f, mean=mean, scale=scale):
            row = row0 + y - 1
            inside = jnp.logical_and(row >= 0, row < height)
            @pl.when(inside)
            def _():
                value = (hid[f, row] - mean) * scale + nbias
                value = 0.5 * value * (1.0 + jnp.tanh(0.5 * value))
                if f < CF:
                    value = value * keep_own
                act[f, y] = value.astype(jnp.bfloat16)

            @pl.when(jnp.logical_not(inside))
            def _():
                act[f, y] = jnp.zeros((width, chans), jnp.bfloat16)

    many = CF * rows_here * width
    for copy in copies:
        copy.wait()
    slabs = []
    weights = []
    for t in range(3):
        for i in range(3):
            tap = 3 * (3 * t + i)
            slabs.append(act[t : t + CF, i : i + rows_here].reshape(many, chans))
            weights.append(jnp.concatenate([mid_w[tap + j] for j in range(3)], axis=1))
    columns = jnp.dot(
        jnp.concatenate(slabs, axis=1),
        jnp.concatenate(weights, axis=0),
        preferred_element_type=jnp.float32,
    ).reshape(CF * rows_here, width, 3 * chans)
    nil = jnp.zeros((1, chans), jnp.float32)
    for f in range(CF):
        for y in range(rows_here):
            part = columns[f * rows_here + y]
            total = hid[outs - CF + f, row0 + y] + mid_b + part[:, chans : 2 * chans]
            total = total + jnp.concatenate([nil, part[:-1, :chans]], axis=0)
            total = total + jnp.concatenate([part[1:, 2 * chans :], nil], axis=0)
            out_ref[f, y] = total.astype(jnp.bfloat16)


def spans(latents, dispatch_plan, span_counts, in_weight, in_bias, norm_gain, norm_bias, mid_weight, mid_bias):
    req_n = lax.axis_size("req")
    row_n = lax.axis_size("row")
    frames, rows_here, lanes = latents.shape[1:]
    chans = in_weight.shape[1]
    frames_in = DEPTH * CF
    outs = frames_in - 2
    height = row_n * rows_here
    blocks = W * C_LAT // LANES
    grant = mid_weight.size * 2 + 4 * chans * W * (outs * height + CF * rows_here)
    grant += 2 * chans * W * outs * (rows_here + 2) + 4 * (frames_in + 1) * (height + 1) * W * LANES
    grant += (8 << 20)
    return pl.pallas_call(
        functools.partial(span_kernel, req_n, row_n),
        out_shape=jax.ShapeDtypeStruct((CF, rows_here, W, chans), jnp.bfloat16),
        in_specs=[pl.BlockSpec(memory_space=pltpu.HBM)] * 9,
        out_specs=pl.BlockSpec(memory_space=pltpu.VMEM),
        scratch_shapes=[
            pltpu.VMEM(latents.shape, latents.dtype),
            pltpu.SMEM(dispatch_plan.shape, jnp.int32),
            pltpu.SMEM(span_counts.shape, jnp.int32),
            pltpu.VMEM(in_weight.shape, in_weight.dtype),
            pltpu.VMEM((chans,), jnp.float32),
            pltpu.VMEM((chans,), jnp.float32),
            pltpu.VMEM((chans,), jnp.float32),
            pltpu.VMEM((chans,), jnp.float32),
            pltpu.VMEM((req_n + DEPTH - 1, rows_here, frames * lanes), latents.dtype),
            pltpu.VMEM((row_n, req_n, DEPTH, rows_here, frames * lanes), latents.dtype),
            pltpu.VMEM(mid_weight.shape, jnp.bfloat16),
            pltpu.VMEM((5 * LANES, chans), jnp.bfloat16),
            pltpu.VMEM((frames_in, height + 1, W, LANES), jnp.bfloat16),
            pltpu.VMEM((frames_in + 1, height + 1, W, LANES), jnp.bfloat16),
            pltpu.VMEM((outs, height, W, chans), jnp.float32),
            pltpu.VMEM((outs, rows_here + 2, W, chans), jnp.bfloat16),
            pltpu.VMEM((blocks * rows_here, LANES), jnp.float32),
            pltpu.VMEM((rows_here, W, LANES), jnp.float32),
            pltpu.SemaphoreType.DMA((17,)),
            pltpu.SemaphoreType.DMA((req_n * row_n,)),
            pltpu.SemaphoreType.DMA((req_n * row_n,)),
        ],
        compiler_params=pltpu.CompilerParams(
            collective_id=0, has_side_effects=True, vmem_limit_bytes=grant
        ),
        name="spans",
    )(
        *(
            pltpu.with_memory_space_constraint(arg, pltpu.HBM)
            for arg in (
                latents,
                dispatch_plan,
                span_counts,
                in_weight,
                in_bias,
                norm_gain,
                norm_bias,
                mid_weight,
                mid_bias,
            )
        )
    )


def local(
    latents,
    dispatch_plan,
    span_counts,
    in_weight,
    in_bias,
    norm_gain,
    norm_bias,
    mid_weight,
    mid_bias,
):
    rows_here = latents.shape[2]
    chans = mid_weight.shape[2]
    mixed = spans(
        latents,
        dispatch_plan,
        span_counts,
        in_weight,
        in_bias,
        norm_gain,
        norm_bias,
        mid_weight,
        mid_bias,
    )
    return mixed.reshape(1, CF, rows_here, W * chans)


def solution(mesh):
    placed = (
        P("groups", None, "row", "req"),
        P("groups"),
        P("groups"),
        P(),
        P(),
        P(),
        P(),
        P(),
        P(),
    )
    return jax.shard_map(
        local,
        mesh=mesh,
        in_specs=placed,
        out_specs=P(("groups", "req"), None, "row", None),
        check_vma=False,
    )
```

```python
import functools

import jax
import jax.numpy as jnp
from jax import lax
from jax.experimental import pallas as pl
from jax.experimental.pallas import tpu as pltpu
from jax.sharding import PartitionSpec as P

C_LAT = 16
G = 32
CF = 2
W = 160
LANES = 128
DEPTH = 3
MESH = pl.DeviceIdType.MESH


def span_kernel(
    req_n,
    row_n,
    lat_hbm,
    plan_hbm,
    counts_hbm,
    in_w_hbm,
    in_b_hbm,
    gain_hbm,
    nbias_hbm,
    mid_w_hbm,
    mid_b_hbm,
    out_ref,
    lat_ref,
    plan_ref,
    counts_ref,
    in_w_ref,
    in_b_ref,
    gain_ref,
    nbias_ref,
    mid_b_ref,
    sel,
    x_ref,
    mid_w,
    in_w,
    pair_rows,
    pair_time,
    hid,
    act,
    lines,
    fanned,
    sems,
    send_sems,
    recv_sems,
):
    me = lax.axis_index("req")
    me_row = lax.axis_index("row")
    devices = req_n * row_n
    flat = me_row * req_n + me
    rows_here = lat_ref.shape[2]
    row0 = me_row * rows_here

    def peer(k):
        target = lax.rem(flat + k, devices)
        return {"row": target // req_n, "req": lax.rem(target, req_n)}

    barrier = pltpu.get_barrier_semaphore()
    for k in range(1, devices):
        pl.semaphore_signal(barrier, inc=1, device_id=peer(k), device_id_type=MESH)
    loads = [
        pltpu.make_async_copy(source, target, sems.at[9 + n])
        for n, (source, target) in enumerate(
            (
                (plan_hbm, plan_ref),
                (lat_hbm, lat_ref),
                (counts_hbm, counts_ref),
                (in_w_hbm, in_w_ref),
                (in_b_hbm, in_b_ref),
                (gain_hbm, gain_ref),
                (nbias_hbm, nbias_ref),
                (mid_b_hbm, mid_b_ref),
            )
        )
    ]
    for load in loads:
        load.start()
    copies = []
    for tap in range(9):
        copy = pltpu.make_async_copy(
            mid_w_hbm.at[pl.ds(3 * tap, 3)], mid_w.at[pl.ds(3 * tap, 3)], sems.at[tap]
        )
        copy.start()
        copies.append(copy)
    loads[0].wait()
    loads[1].wait()
    for d in range(DEPTH - 1):
        sel[d] = jnp.zeros_like(sel[d])
    for d in range(req_n):
        span = lat_ref[plan_ref[d]].astype(jnp.float32)
        sel[d + DEPTH - 1] = jnp.concatenate([span[f] for f in range(CF)], axis=1).astype(sel.dtype)
    pl.semaphore_wait(barrier, devices - 1)
    sends = []
    for k in range(1, devices):
        where = peer(k)
        send = pltpu.make_async_remote_copy(
            src_ref=sel.at[pl.ds(where["req"], DEPTH)],
            dst_ref=x_ref.at[me_row, me],
            send_sem=send_sems.at[k],
            recv_sem=recv_sems.at[k],
            device_id=where,
            device_id_type=MESH,
        )
        send.start()
        sends.append(send)
    x_ref[me_row, me] = sel[pl.ds(me, DEPTH)]
    for load in loads[2:]:
        load.wait()

    frames_in = DEPTH * CF
    height = row_n * rows_here
    lanes = x_ref.shape[4] // CF
    width = req_n * lanes // C_LAT
    blocks = width * C_LAT // LANES
    chans = in_w_ref.shape[1]
    outs = frames_in - 2
    in_b = in_b_ref[...].reshape(1, chans)
    gain = gain_ref[...].reshape(1, chans)
    nbias = nbias_ref[...].reshape(1, chans)
    mid_b = mid_b_ref[...].reshape(1, chans)
    def keep_of(d):
        start = jnp.int32(0)
        first = d <= 0
        for r in range(counts_ref.shape[0]):
            first = jnp.logical_or(first, start == d)
            start = start + counts_ref[r]
        return jnp.where(first, 0.0, 1.0).astype(jnp.float32)

    keep_own = keep_of(me)
    keep_prev = keep_of(me - 1)

    half = LANES // 2
    three = 3 * C_LAT
    in_w[...] = jnp.zeros_like(in_w)
    for t in range(3):
        for i in range(3):
            if i < 2:
                base = t * LANES + i * half
            else:
                base = 3 * LANES + t * half
            in_w[base : base + three, :] = in_w_ref[(3 * t + i) * three : (3 * t + i + 1) * three, :]

    zero_slab = jnp.zeros((width, LANES), jnp.bfloat16)
    for f in range(frames_in):
        pair_rows[f, 0] = zero_slab
    for f in range(frames_in + 1):
        pair_time[f, height] = zero_slab
    for y in range(height):
        pair_time[frames_in, y] = zero_slab

    lane = lax.broadcasted_iota(jnp.int32, (blocks, LANES), 1)
    low = lane < C_LAT
    high = jnp.logical_and(lane >= 2 * C_LAT, lane < three)
    left = lane < half
    nothing = jnp.zeros((1, LANES), jnp.float32)

    def place_row(f, y, here):
        cells = lines[pl.ds(here, blocks, stride=rows_here), :]
        turned = [pltpu.roll(cells, (C_LAT - C_LAT * p) % LANES, 1) if p != 1 else cells for p in range(8)]
        for p in range(8):
            window = turned[p]
            other = turned[(p + 4) % 8]
            if p == 0:
                before = jnp.concatenate([nothing, window[:-1]], axis=0)
                window = jnp.where(low, before, window)
                other = pltpu.roll(window, half, 1)
            if p == 7:
                after = jnp.concatenate([window[1:], nothing], axis=0)
                window = jnp.where(high, after, window)
                other = pltpu.roll(window, half, 1)
            fanned[here, pl.ds(p, blocks, stride=8), :] = jnp.where(left, window, other)
        both = fanned[here].astype(jnp.bfloat16)
        pair_rows[f, y + 1, :, :half] = both[:, :half]
        pair_rows[f, y, :, half:] = both[:, half:]
        pair_time[f + 1, y, :, :half] = both[:, :half]
        pair_time[f, y, :, half:] = both[:, half:]

    for send in sends:
        send.wait()

    @pl.loop(0, DEPTH)
    def _(span):
        keep = jnp.where(span == 0, keep_prev, jnp.where(span == 1, keep_own, 1.0))

        @pl.loop(0, row_n)
        def _(r):
            shards = [x_ref[r, q, span].astype(jnp.float32) * keep for q in range(req_n)]
            for frame in range(CF):
                merged = jnp.concatenate(
                    [shard[:, frame * lanes : (frame + 1) * lanes] for shard in shards], axis=1
                )
                for b in range(blocks):
                    lines[b * rows_here : (b + 1) * rows_here, :] = merged[:, b * LANES : (b + 1) * LANES]
                for here in range(rows_here):
                    place_row(span * CF + frame, r * rows_here + here, here)

    sums = []
    cells = height * width
    for f in range(outs):
        taps = [
            pair_rows[f, :height],
            pair_rows[f + 1, :height],
            pair_rows[f + 2, :height],
            pair_time[f + 1, 1:],
            pair_time[f + 3, 1:],
        ]
        stacked = jnp.concatenate([tap.reshape(cells, LANES) for tap in taps], axis=1)
        hidden = jnp.dot(stacked, in_w[...], preferred_element_type=jnp.float32) + in_b
        hid[f] = hidden.reshape(height, width, chans)
        sums.append(jnp.sum(hidden, axis=0, keepdims=True))
        sums.append(jnp.sum(hidden * hidden, axis=0, keepdims=True))
    per_group = chans // G
    down = lax.broadcasted_iota(jnp.int32, (chans, chans), 0) // per_group
    over = lax.broadcasted_iota(jnp.int32, (chans, chans), 1) // per_group
    same = jnp.where(down == over, 1.0, 0.0).astype(jnp.bfloat16)
    stats = jnp.concatenate(sums, axis=0)
    parts = []
    for _ in range(3):
        part = stats.astype(jnp.bfloat16)
        parts.append(part)
        stats = stats - part.astype(jnp.float32)
    grouped = sum(jnp.dot(part, same, preferred_element_type=jnp.float32) for part in reversed(parts))
    grouped = grouped / (cells * per_group)

    span_rows = rows_here + 2
    for f in range(outs):
        mean = grouped[2 * f : 2 * f + 1]
        var = grouped[2 * f + 1 : 2 * f + 2] - mean * mean
        scale = lax.rsqrt(var + 1e-06) * gain

        @pl.loop(0, span_rows)
        def _(y, f=f, mean=mean, scale=scale):
            row = row0 + y - 1
            inside = jnp.logical_and(row >= 0, row < height)
            @pl.when(inside)
            def _():
                value = (hid[f, row] - mean) * scale + nbias
                value = 0.5 * value * (1.0 + jnp.tanh(0.5 * value))
                if f < CF:
                    value = value * keep_own
                act[f, y] = value.astype(jnp.bfloat16)

            @pl.when(jnp.logical_not(inside))
            def _():
                act[f, y] = jnp.zeros((width, chans), jnp.bfloat16)

    many = CF * rows_here * width
    for copy in copies:
        copy.wait()
    slabs = []
    weights = []
    for t in range(3):
        for i in range(3):
            tap = 3 * (3 * t + i)
            slabs.append(act[t : t + CF, i : i + rows_here].reshape(many, chans))
            weights.append(jnp.concatenate([mid_w[tap + j] for j in range(3)], axis=1))
    columns = jnp.dot(
        jnp.concatenate(slabs, axis=1),
        jnp.concatenate(weights, axis=0),
        preferred_element_type=jnp.float32,
    ).reshape(CF * rows_here, width, 3 * chans)
    nil = jnp.zeros((1, chans), jnp.float32)
    for f in range(CF):
        for y in range(rows_here):
            part = columns[f * rows_here + y]
            total = hid[outs - CF + f, row0 + y] + mid_b + part[:, chans : 2 * chans]
            total = total + jnp.concatenate([nil, part[:-1, :chans]], axis=0)
            total = total + jnp.concatenate([part[1:, 2 * chans :], nil], axis=0)
            out_ref[f, y] = total.astype(jnp.bfloat16)


def spans(latents, dispatch_plan, span_counts, in_weight, in_bias, norm_gain, norm_bias, mid_weight, mid_bias):
    req_n = lax.axis_size("req")
    row_n = lax.axis_size("row")
    frames, rows_here, lanes = latents.shape[1:]
    chans = in_weight.shape[1]
    frames_in = DEPTH * CF
    outs = frames_in - 2
    height = row_n * rows_here
    blocks = W * C_LAT // LANES
    grant = mid_weight.size * 2 + 4 * chans * W * (outs * height + CF * rows_here)
    grant += 2 * chans * W * outs * (rows_here + 2) + 4 * (frames_in + 1) * (height + 1) * W * LANES
    grant += (8 << 20)
    return pl.pallas_call(
        functools.partial(span_kernel, req_n, row_n),
        out_shape=jax.ShapeDtypeStruct((CF, rows_here, W, chans), jnp.bfloat16),
        in_specs=[pl.BlockSpec(memory_space=pltpu.HBM)] * 9,
        out_specs=pl.BlockSpec(memory_space=pltpu.VMEM),
        scratch_shapes=[
            pltpu.VMEM(latents.shape, latents.dtype),
            pltpu.SMEM(dispatch_plan.shape, jnp.int32),
            pltpu.SMEM(span_counts.shape, jnp.int32),
            pltpu.VMEM(in_weight.shape, in_weight.dtype),
            pltpu.VMEM((chans,), jnp.float32),
            pltpu.VMEM((chans,), jnp.float32),
            pltpu.VMEM((chans,), jnp.float32),
            pltpu.VMEM((chans,), jnp.float32),
            pltpu.VMEM((req_n + DEPTH - 1, rows_here, frames * lanes), latents.dtype),
            pltpu.VMEM((row_n, req_n, DEPTH, rows_here, frames * lanes), latents.dtype),
            pltpu.VMEM(mid_weight.shape, jnp.bfloat16),
            pltpu.VMEM((5 * LANES, chans), jnp.bfloat16),
            pltpu.VMEM((frames_in, height + 1, W, LANES), jnp.bfloat16),
            pltpu.VMEM((frames_in + 1, height + 1, W, LANES), jnp.bfloat16),
            pltpu.VMEM((outs, height, W, chans), jnp.float32),
            pltpu.VMEM((outs, rows_here + 2, W, chans), jnp.bfloat16),
            pltpu.VMEM((blocks * rows_here, LANES), jnp.float32),
            pltpu.VMEM((rows_here, W, LANES), jnp.float32),
            pltpu.SemaphoreType.DMA((17,)),
            pltpu.SemaphoreType.DMA((req_n * row_n,)),
            pltpu.SemaphoreType.DMA((req_n * row_n,)),
        ],
        compiler_params=pltpu.CompilerParams(
            collective_id=0, has_side_effects=True, vmem_limit_bytes=grant
        ),
        name="spans",
    )(
        *(
            pltpu.with_memory_space_constraint(arg, pltpu.HBM)
            for arg in (
                latents,
                dispatch_plan,
                span_counts,
                in_weight,
                in_bias,
                norm_gain,
                norm_bias,
                mid_weight,
                mid_bias,
            )
        )
    )


def local(
    latents,
    dispatch_plan,
    span_counts,
    in_weight,
    in_bias,
    norm_gain,
    norm_bias,
    mid_weight,
    mid_bias,
):
    rows_here = latents.shape[2]
    chans = mid_weight.shape[2]
    mixed = spans(
        latents,
        dispatch_plan,
        span_counts,
        in_weight,
        in_bias,
        norm_gain,
        norm_bias,
        mid_weight,
        mid_bias,
    )
    return mixed.reshape(1, CF, rows_here, W * chans)


def solution(mesh):
    placed = (
        P("groups", None, "row", "req"),
        P("groups"),
        P("groups"),
        P(),
        P(),
        P(),
        P(),
        P(),
        P(),
    )
    return jax.shard_map(
        local,
        mesh=mesh,
        in_specs=placed,
        out_specs=P(("groups", "req"), None, "row", None),
        check_vma=False,
    )
```
